32 devices in a mesh: blk: 16 (over z, y, x), grp: 2 (over core).
Axes of the slice: x: 2, y: 2, z: 4, core: 2. Of those that a mesh axis runs over, the one named last changes fastest.
Arguments:
- item_start: bfloat16 [4096, 128], P(('blk', 'grp')), may hold values from -0.5 to 0.5
- ratings: bfloat16 [4, 1024, 256], P(None, 'blk', 'grp'), may hold values from -6 to 6
- rating_bits: int32 [4, 1024], P(None, 'blk'), may hold values from -2147483648 to 2147483647, as said below
- plan: int32 [4], replicated, may hold values from 1 to 15, as said below
Outputs:
- user_factors: bfloat16 [1024, 128], P(('blk', 'grp'))
- item_factors: bfloat16 [4096, 128], P(('blk', 'grp'))
The draws below stay inside these ranges and needn't reach their ends.
Inputs may be any that keep to these rules, and one draw needn't show every extreme that they name: `plan`: the 4 offsets are distinct, and among them are 15 and 8. `rating_bits`: every word has a set bit among bits 0 to 15 and one among bits 16 to 31.
All inputs are finite; a program needn't handle non-finite values. Where the reference program divides by a largest or mean magnitude, that divisor is 1e-20 or more.
Results may differ from the reference program's by a relative error of at most 0.015.
Values may be sent and summed in bfloat16 or wider, within the bound.
A program may use at most 64 MiB of HBM per device.

```python
import jax
import jax.numpy as jnp
from jax import lax

R = 128
UB = 64
IB = 256
KS = 4
SWEEPS = 4
NB = 16
USERS = 1024
ITEMS = 4096


def draw_rating_bits(key, part):
    shape = (KS, NB * UB)
    first_key = jax.random.fold_in(key, 11)
    second_key = jax.random.fold_in(key, 12)
    low_key = jax.random.fold_in(key, 13)
    high_key = jax.random.fold_in(key, 14)
    first_word = jax.random.randint(first_key, shape, -2147483648, 2147483647, dtype=jnp.int32)
    second_word = jax.random.randint(second_key, shape, -2147483648, 2147483647, dtype=jnp.int32)
    low_bit = jax.random.randint(low_key, shape, 0, 16, dtype=jnp.int32)
    high_bit = jax.random.randint(high_key, shape, 16, 32, dtype=jnp.int32)
    single = jnp.ones(shape, jnp.int32)
    return first_word | second_word | jnp.left_shift(single, low_bit) | jnp.left_shift(single, high_bit)


def draw_plan(key, part):
    half_block = NB // 2
    order = jax.random.permutation(jax.random.fold_in(key, 21), NB - 3).astype(jnp.int32)
    others = order[:KS - 2] + 1
    others = jnp.where(others >= half_block, others + 1, others)
    fixed_pair = jnp.array([NB - 1, half_block], dtype=jnp.int32)
    offsets = jnp.concatenate([fixed_pair, others.astype(jnp.int32)])
    placing = jax.random.permutation(jax.random.fold_in(key, 22), KS)
    return offsets[placing].astype(jnp.int32)


def block_scale(stream_key, shape, pieces, smallest, top_value):
    def one(axis_at, parts):
        heights = jax.random.uniform(jax.random.fold_in(jax.random.fold_in(stream_key, 6), axis_at), (parts,), jnp.float32, smallest / len(pieces), top_value / len(pieces))
        return jnp.repeat(jnp.exp(heights), shape[axis_at] // parts).reshape((-1,) + (1,) * (len(shape) - axis_at - 1))

    loudness = one(*pieces[0])
    for cut in pieces[1:]:
        loudness = loudness * one(*cut)
    return loudness


def centred(stream_key, extent, deviation, bound, split=(), kind=jnp.bfloat16):
    loudness = block_scale(stream_key, extent, split, -0.22, 0.18) if split else 1.0
    values = jax.random.normal(stream_key, extent, jnp.float32) * deviation * loudness
    return jnp.minimum(jnp.maximum(values, -bound), bound).astype(kind)


def setup_inputs(seed: int = 0) -> dict:
    key_of = jax.random.split(jax.random.key(seed), 5)
    item_start = centred(key_of[0], (ITEMS, R), R ** -0.5, 0.5, ((0, 32),))
    ratings = centred(key_of[1], (KS, USERS, IB), 1.0, 6.0, ((1, 16), (2, 2)))
    rating_bits = draw_rating_bits(jax.random.fold_in(key_of[4], 71), 0)
    plan = draw_plan(jax.random.fold_in(key_of[4], 71), 0)
    return {"item_start": item_start, "ratings": ratings, "rating_bits": rating_bits, "plan": plan}


ridge_scale = 0.005


def expand_bits(bitmaps, first_bit, bit_count, group_width):
    shifts = first_bit + jnp.arange(bit_count, dtype=jnp.int32)
    bit_values = jnp.right_shift(bitmaps[..., None], shifts) & 1
    spread = jnp.broadcast_to(bit_values[..., None], bit_values.shape + (group_width,))
    return spread.reshape(bitmaps.shape + (bit_count * group_width,)).astype(jnp.bfloat16)


def row_terms(indicator, rating_rows, factors):
    row_count = indicator.shape[0]
    rank_width = factors.shape[1]
    weighted = indicator[:, None, :] * factors.T[None, :, :]
    gram_sum = jnp.dot(weighted.reshape(row_count * rank_width, -1), factors, preferred_element_type=jnp.float32)
    gram_sum = gram_sum.reshape(row_count, rank_width, rank_width)
    right_side = jnp.dot(indicator * rating_rows, factors, preferred_element_type=jnp.float32)
    rated_count = jnp.sum(indicator.astype(jnp.float32), axis=1)
    return gram_sum, right_side, rated_count


def solve_rows(gram_sum, right_side, rated_count):
    rank_width = gram_sum.shape[1]
    ridge_term = ridge_scale * (rated_count + 1.0)
    identity_mat = jnp.eye(rank_width, dtype=jnp.float32)
    system = gram_sum + ridge_term[:, None, None] * identity_mat
    row_bound = jnp.max(jnp.sum(jnp.abs(system), axis=2), axis=1)
    answer = jnp.zeros_like(right_side)
    for sweep_step in range(SWEEPS):
        applied = jnp.einsum('urs,us->ur', system, answer, precision=lax.Precision.HIGHEST)
        answer = answer + (right_side - applied) / row_bound[:, None]
    return answer.astype(jnp.bfloat16)


def user_sweep(item_rows, ratings, indicators, plan):
    def solve_block(block_id):
        totals = None
        for k in range(KS):
            source = (block_id + plan[k]) % NB
            factors = lax.dynamic_slice_in_dim(item_rows, (source * IB).astype(jnp.int32), IB, 0)
            start_row = (block_id * UB).astype(jnp.int32)
            indicator = lax.dynamic_slice_in_dim(indicators[k], start_row, UB, 0)
            rating_rows = lax.dynamic_slice_in_dim(ratings[k], start_row, UB, 0)
            terms = row_terms(indicator, rating_rows, factors)
            totals = terms if totals is None else tuple(a + b for a, b in zip(totals, terms))
        return solve_rows(*totals)
    solved = lax.map(solve_block, jnp.arange(NB, dtype=jnp.int32))
    return solved.reshape(NB * UB, -1)


def item_sweep(user_rows, ratings, indicators, plan):
    def solve_block(block_id):
        totals = None
        for k in range(KS):
            source = (block_id - plan[k]) % NB
            start_row = (source * UB).astype(jnp.int32)
            factors = lax.dynamic_slice_in_dim(user_rows, start_row, UB, 0)
            indicator = lax.dynamic_slice_in_dim(indicators[k], start_row, UB, 0)
            rating_rows = lax.dynamic_slice_in_dim(ratings[k], start_row, UB, 0)
            terms = row_terms(indicator.T, rating_rows.T, factors)
            totals = terms if totals is None else tuple(a + b for a, b in zip(totals, terms))
        return solve_rows(*totals)
    solved = lax.map(solve_block, jnp.arange(NB, dtype=jnp.int32))
    return solved.reshape(NB * IB, -1)


def reference(item_start, ratings, rating_bits, plan):
    indicators = expand_bits(rating_bits, 0, 32, IB // 32)
    first_users = user_sweep(item_start, ratings, indicators, plan)
    item_factors = item_sweep(first_users, ratings, indicators, plan)
    user_factors = user_sweep(item_factors, ratings, indicators, plan)
    return user_factors, item_factors
```

```python
import functools

import jax
import jax.numpy as jnp
from jax import lax
from jax.experimental import pallas as pl
from jax.experimental.pallas import tpu as pltpu
from jax.sharding import PartitionSpec as P

SWEEPS = 4
WORD = 32
ridge_scale = 0.005
MESH = pl.DeviceIdType.MESH
VMEM = pl.BlockSpec(memory_space=pltpu.VMEM)
SMEM = pl.BlockSpec(memory_space=pltpu.SMEM)
F32 = jnp.float32
BF16 = jnp.bfloat16


def halves(value):
    high = value.astype(BF16)
    return high, (value - high.astype(F32)).astype(BF16)


def dot(a, b):
    return jnp.dot(a, b, preferred_element_type=F32)


def dot_nt(a, b):
    return lax.dot_general(a, b, (((1,), (1,)), ((), ())), preferred_element_type=F32)


def dot_tn(a, b):
    return lax.dot_general(a, b, (((0,), (0,)), ((), ())), preferred_element_type=F32)


def relax(factors, mask, right, count, bound):
    rows = right.shape[0]
    ridge = ridge_scale * (count + 1.0)
    inverse = 1.0 / bound
    answer = right * inverse
    for _ in range(SWEEPS - 1):
        high, low = halves(answer)
        seen = dot_nt(jnp.concatenate([high, low], axis=0), factors)
        seen = (seen[:rows] + seen[rows:]) * mask
        high, low = halves(seen)
        applied = dot(jnp.concatenate([high, low], axis=0), factors)
        applied = applied[:rows] + applied[rows:] + ridge * answer
        answer = answer + (right - applied) * inverse
    return answer.astype(BF16)


def prep_kernel(plan_ref, ratings_ref, bits_ref, bits_t_ref, send_ref, masked_ref, mask_ref):
    tiles, users, width = ratings_ref.shape
    groups = WORD // 2
    span = width // groups
    own = lax.axis_index("grp")
    half_users = users // 2
    send_ref[...] = jnp.zeros_like(send_ref)
    group_at = lax.broadcasted_iota(jnp.int32, (users, width), 1) // span + own * groups
    row_at = lax.broadcasted_iota(jnp.int32, (groups, users), 0) + own * groups
    item_at = lax.broadcasted_iota(jnp.int32, (half_users, 2 * width), 1) // span
    my_first = pl.multiple_of(own * half_users, half_users)
    for k in range(tiles):
        column = bits_t_ref[:, k:k + 1]
        shown = (jnp.right_shift(jnp.broadcast_to(column, (users, width)), group_at) & 1).astype(F32)
        masked = (ratings_ref[k].astype(F32) * shown).astype(BF16)
        masked_ref[k] = masked
        words = jnp.broadcast_to(bits_ref[k:k + 1, :], (groups, users))
        grouped = (jnp.right_shift(words, row_at) & 1).astype(F32).astype(BF16)
        offset = plan_ref[k]
        send_ref[offset, 0:users, :] = masked
        send_ref[offset, users:users + groups, 0:users] = grouped
        mine = bits_t_ref[pl.ds(my_first, half_users), k:k + 1]
        seen = jnp.right_shift(jnp.broadcast_to(mine, (half_users, 2 * width)), item_at) & 1
        mask_ref[:, k * 2 * width:(k + 1) * 2 * width] = seen.astype(F32).astype(BF16)


def gather_steps(blocks, lo, x_ref, out_ref, ssem, rsem, psem, prsem, lsem):
    me = lax.axis_index("blk")
    g = lax.axis_index("grp")
    hi = blocks // lo
    mh, ml = me // lo, me % lo
    sends = []

    def put(src, slot, device, send_sem, recv_sem):
        copy = pltpu.make_async_remote_copy(
            src_ref=src, dst_ref=out_ref.at[2 * slot + g], send_sem=send_sem, recv_sem=recv_sem,
            device_id=device, device_id_type=MESH)
        copy.start()
        sends.append(copy)

    def spread(src, slot, d):
        for e in range(1, lo):
            put(src, slot, (mh * lo + (ml + e) % lo, g), ssem.at[hi + d * lo + e], rsem.at[slot])

    def partner(src, slot, at):
        put(src, slot, (me, 1 - g), psem.at[at], prsem.at[slot])

    def arrived(slot, sem):
        pltpu.make_async_remote_copy(
            src_ref=x_ref, dst_ref=out_ref.at[2 * slot + g], send_sem=ssem.at[0], recv_sem=sem,
            device_id=(me, 1 - g), device_id_type=MESH).wait_recv()

    for d in range(1, hi):
        put(x_ref, me, (((mh + d) % hi) * lo + ml, g), ssem.at[d], rsem.at[me])
    spread(x_ref, me, 0)
    partner(x_ref, me, 0)
    local = pltpu.make_async_copy(x_ref, out_ref.at[2 * me + g], lsem)
    local.start()

    def finish():
        at = 1
        for d in range(1, hi):
            slot = ((mh + hi - d) % hi) * lo + ml
            arrived(slot, rsem.at[slot])
            spread(out_ref.at[2 * slot + g], slot, d)
            partner(out_ref.at[2 * slot + g], slot, at)
            at += 1
        for d in range(hi):
            for e in range(1, lo):
                slot = ((mh + hi - d) % hi) * lo + (ml + lo - e) % lo
                arrived(slot, rsem.at[slot])
                partner(out_ref.at[2 * slot + g], slot, at)
                at += 1
        for slot in range(blocks):
            pltpu.make_async_remote_copy(
                src_ref=x_ref, dst_ref=out_ref.at[2 * slot + 1 - g], send_sem=ssem.at[0],
                recv_sem=prsem.at[slot], device_id=(me, 1 - g), device_id_type=MESH).wait_recv()
        for copy in sends:
            copy.wait_send()
        local.wait()

    return finish


def greet_gather(blocks, lo):
    me = lax.axis_index("blk")
    g = lax.axis_index("grp")
    hi = blocks // lo
    mh, ml = me // lo, me % lo
    barrier = pltpu.get_barrier_semaphore()
    for d in range(1, hi):
        pl.semaphore_signal(barrier, inc=1, device_id=(((mh + d) % hi) * lo + ml, g), device_id_type=MESH)
    for e in range(1, lo):
        pl.semaphore_signal(barrier, inc=1, device_id=(mh * lo + (ml + e) % lo, g), device_id_type=MESH)
    pl.semaphore_signal(barrier, inc=1, device_id=(me, 1 - g), device_id_type=MESH)
    pl.semaphore_wait(barrier, hi - 1 + lo - 1 + 1)


def greet_all(blocks):
    me = lax.axis_index("blk")
    g = lax.axis_index("grp")
    barrier = pltpu.get_barrier_semaphore()
    for o in range(1, blocks):
        pl.semaphore_signal(barrier, inc=1, device_id=((me + o) % blocks, g), device_id_type=MESH)
    pl.semaphore_signal(barrier, inc=1, device_id=(me, 1 - g), device_id_type=MESH)
    pl.semaphore_wait(barrier, blocks)


def gather_kernel(blocks, lo, x_ref, out_ref, ssem, rsem, psem, prsem, lsem):
    greet_gather(blocks, lo)
    gather_steps(blocks, lo, x_ref, out_ref, ssem, rsem, psem, prsem, lsem)()


def first_kernel(blocks, lo, x_ref, send_ref, masked_ref, out_ref, slots_ref, other_ref,
                 ssem, rsem, psem, prsem, lsem, a_send, a_recv, m_send, m_recv):
    me = lax.axis_index("blk")
    g = lax.axis_index("grp")
    greet_all(blocks)
    half = other_ref.shape[1]
    finish = gather_steps(blocks, lo, x_ref, out_ref, ssem, rsem, psem, prsem, lsem)
    swap = pltpu.make_async_remote_copy(
        src_ref=masked_ref.at[:, pl.ds(pl.multiple_of((1 - g) * half, half), half), :], dst_ref=other_ref,
        send_sem=m_send, recv_sem=m_recv, device_id=(me, 1 - g), device_id_type=MESH)
    swap.start()
    moves = []
    for o in range(1, blocks):
        copy = pltpu.make_async_remote_copy(
            src_ref=send_ref.at[o], dst_ref=slots_ref.at[o], send_sem=a_send.at[o], recv_sem=a_recv.at[o],
            device_id=((me + o) % blocks, g), device_id_type=MESH)
        copy.start()
        moves.append(copy)
    finish()
    swap.wait()
    for copy in moves:
        copy.wait()


def user_kernel(blocks, plan_ref, items_ref, mask_ref, masked_ref, other_ref, out_ref, vt_ref, v_ref, sums_ref):
    me = lax.axis_index("blk")
    g = lax.axis_index("grp")
    tiles, half, width = other_ref.shape
    rank = items_ref.shape[2]
    mine = pl.multiple_of(g * half, half)
    pieces = []
    for k in range(tiles):
        source = (me + plan_ref[k]) % blocks
        for part in range(2):
            block = items_ref[2 * source + part]
            at = (2 * k + part) * width
            v_ref[at:at + width, :] = block
            vt_ref[:, at:at + width] = block.astype(F32).T.astype(BF16)
        own = masked_ref[k, pl.ds(mine, half), :].astype(F32)
        far = other_ref[k].astype(F32)
        pieces.append(jnp.where(g == 0, own, far).astype(BF16))
        pieces.append(jnp.where(g == 0, far, own).astype(BF16))
    factors = v_ref[...]
    mask = mask_ref[...].astype(F32)
    count = jnp.sum(mask, axis=1, keepdims=True)
    ridge = ridge_scale * (count + 1.0)
    right = dot(jnp.concatenate(pieces, axis=1), factors)
    diagonal = (lax.broadcasted_iota(jnp.int32, (rank, rank), 0)
                == lax.broadcasted_iota(jnp.int32, (rank, rank), 1)).astype(F32)
    turned = vt_ref[...]
    for u in range(half):
        weighted = turned * mask_ref[u:u + 1, :]
        gram = dot(weighted, factors) + ridge[u:u + 1, :] * diagonal
        sums_ref[u:u + 1, :] = jnp.sum(jnp.abs(gram), axis=0, keepdims=True)
    bound = jnp.max(sums_ref[...], axis=1, keepdims=True)
    out_ref[...] = relax(factors, mask, right, count, bound)


def item_kernel(blocks, plan_ref, users_ref, slots_ref, out_ref, mask_ref, sums_ref):
    me = lax.axis_index("blk")
    tiles = plan_ref.shape[0]
    items = out_ref.shape[0]
    rank = users_ref.shape[2]
    half = users_ref.shape[1]
    users = 2 * half
    groups = slots_ref.shape[1] - users
    span = items // groups
    factor_list, rating_list, mask_list = [], [], []
    for k in range(tiles):
        offset = plan_ref[k]
        source = (me + blocks - offset) % blocks
        factor_list += [users_ref[2 * source], users_ref[2 * source + 1]]
        rating_list.append(slots_ref[offset, 0:users, :])
        mask_list.append(slots_ref[offset, users:users + groups, 0:users].astype(F32))
    factors = jnp.concatenate(factor_list, axis=0)
    right = dot_tn(jnp.concatenate(rating_list, axis=0), factors)
    mask_ref[...] = jnp.concatenate(mask_list, axis=1)
    turned = factors.astype(F32).T.astype(BF16)
    diagonal = (lax.broadcasted_iota(jnp.int32, (rank, rank), 0)
                == lax.broadcasted_iota(jnp.int32, (rank, rank), 1)).astype(F32)
    spread = []
    for j in range(groups):
        row = mask_ref[j:j + 1, :]
        ridge = ridge_scale * (jnp.sum(row, axis=1, keepdims=True) + 1.0)
        gram = dot(turned * row.astype(BF16), factors) + ridge * diagonal
        sums_ref[j * span:(j + 1) * span, :] = jnp.broadcast_to(
            jnp.sum(jnp.abs(gram), axis=0, keepdims=True), (span, rank))
        spread.append(jnp.broadcast_to(row, (span, row.shape[1])))
    mask = jnp.concatenate(spread, axis=0)
    count = jnp.sum(mask, axis=1, keepdims=True)
    bound = jnp.max(sums_ref[...], axis=1, keepdims=True)
    out_ref[...] = relax(factors, mask, right, count, bound)


def shaped(shape, dtype=BF16):
    return jax.ShapeDtypeStruct(shape, dtype)


def gather_sems(blocks, lo):
    dma = pltpu.SemaphoreType.DMA
    hi = blocks // lo
    return [dma((hi + hi * lo,)), dma((blocks,)), dma((blocks,)), dma((blocks,)), dma(())]


def gather(value, blocks, lo, identity):
    return pl.pallas_call(
        functools.partial(gather_kernel, blocks, lo),
        out_shape=shaped((2 * blocks,) + value.shape),
        in_specs=[VMEM], out_specs=VMEM,
        scratch_shapes=gather_sems(blocks, lo),
        compiler_params=pltpu.CompilerParams(collective_id=identity, has_side_effects=True),
        name="gather_%d" % identity,
    )(value)


def body(item_start, ratings, rating_bits, plan):
    blocks = lax.axis_size("blk")
    lo = 4 if blocks % 4 == 0 else 1
    tiles, users, width = ratings.shape
    rank = item_start.shape[1]
    half = users // 2
    groups = WORD // 2
    dma = pltpu.SemaphoreType.DMA
    slot = (users + groups, width)
    send, masked, mask = pl.pallas_call(
        prep_kernel,
        out_shape=(shaped((blocks,) + slot), shaped(ratings.shape), shaped((half, tiles * 2 * width))),
        in_specs=[SMEM, VMEM, VMEM, VMEM], out_specs=(VMEM, VMEM, VMEM),
        name="prep",
    )(plan, ratings, rating_bits, rating_bits.T)
    gathered, slots, other = pl.pallas_call(
        functools.partial(first_kernel, blocks, lo),
        out_shape=(shaped((2 * blocks,) + item_start.shape), shaped((blocks,) + slot),
                   shaped((tiles, half, width))),
        in_specs=[VMEM] * 3, out_specs=(VMEM,) * 3,
        scratch_shapes=gather_sems(blocks, lo) + [dma((blocks,)), dma((blocks,)), dma(()), dma(())],
        compiler_params=pltpu.CompilerParams(collective_id=0, has_side_effects=True),
        name="first_gather",
    )(item_start, send, masked)

    def user_pass(factors):
        return pl.pallas_call(
            functools.partial(user_kernel, blocks),
            out_shape=shaped((half, rank)),
            in_specs=[SMEM] + [VMEM] * 4, out_specs=VMEM,
            scratch_shapes=[pltpu.VMEM((rank, tiles * 2 * width), BF16),
                            pltpu.VMEM((tiles * 2 * width, rank), BF16), pltpu.VMEM((half, rank), F32)],
            name="user_pass",
        )(plan, factors, mask, masked, other)

    first_users = user_pass(gathered)
    all_users = gather(first_users, blocks, lo, 1)
    item_factors = pl.pallas_call(
        functools.partial(item_kernel, blocks),
        out_shape=shaped(item_start.shape),
        in_specs=[SMEM, VMEM, VMEM], out_specs=VMEM,
        scratch_shapes=[pltpu.VMEM((groups, tiles * users), F32), pltpu.VMEM(item_start.shape, F32)],
        name="item_pass",
    )(plan, all_users, slots)
    user_factors = user_pass(gather(item_factors, blocks, lo, 2))
    return (user_factors, item_factors)


def solution(mesh):
    in_specs = (P(("blk", "grp"), None), P(None, "blk", "grp"), P(None, "blk"), P())
    out_specs = (P(("blk", "grp"), None), P(("blk", "grp"), None))
    return jax.shard_map(body, mesh=mesh, in_specs=in_specs, out_specs=out_specs, check_vma=False)
```

```python
import functools

import jax
import jax.numpy as jnp
from jax import lax
from jax.experimental import pallas as pl
from jax.experimental.pallas import tpu as pltpu
from jax.sharding import PartitionSpec as P

SWEEPS = 4
WORD = 32
ridge_scale = 0.005
MESH = pl.DeviceIdType.MESH
VMEM = pl.BlockSpec(memory_space=pltpu.VMEM)
SMEM = pl.BlockSpec(memory_space=pltpu.SMEM)
F32 = jnp.float32
BF16 = jnp.bfloat16


def halves(value):
    high = value.astype(BF16)
    return high, (value - high.astype(F32)).astype(BF16)


def dot(a, b):
    return jnp.dot(a, b, preferred_element_type=F32)


def dot_nt(a, b):
    return lax.dot_general(a, b, (((1,), (1,)), ((), ())), preferred_element_type=F32)


def dot_tn(a, b):
    return lax.dot_general(a, b, (((0,), (0,)), ((), ())), preferred_element_type=F32)


def relax(factors, mask, right, count, bound):
    rows = right.shape[0]
    ridge = ridge_scale * (count + 1.0)
    inverse = 1.0 / bound
    answer = right * inverse
    for _ in range(SWEEPS - 1):
        high, low = halves(answer)
        seen = dot_nt(jnp.concatenate([high, low], axis=0), factors)
        seen = (seen[:rows] + seen[rows:]) * mask
        high, low = halves(seen)
        applied = dot(jnp.concatenate([high, low], axis=0), factors)
        applied = applied[:rows] + applied[rows:] + ridge * answer
        answer = answer + (right - applied) * inverse
    return answer.astype(BF16)


def gather_steps(blocks, lo, x_ref, out_ref, ssem, rsem, psem, prsem, lsem):
    me = lax.axis_index("blk")
    g = lax.axis_index("grp")
    hi = blocks // lo
    mh, ml = me // lo, me % lo
    sends = []

    def put(src, slot, device, send_sem, recv_sem):
        copy = pltpu.make_async_remote_copy(
            src_ref=src, dst_ref=out_ref.at[2 * slot + g], send_sem=send_sem, recv_sem=recv_sem,
            device_id=device, device_id_type=MESH)
        copy.start()
        sends.append(copy)

    def spread(src, slot, d):
        for e in range(1, lo):
            put(src, slot, (mh * lo + (ml + e) % lo, g), ssem.at[hi + d * lo + e], rsem.at[slot])

    def partner(src, slot, at):
        put(src, slot, (me, 1 - g), psem.at[at], prsem.at[slot])

    def arrived(slot, sem):
        pltpu.make_async_remote_copy(
            src_ref=x_ref, dst_ref=out_ref.at[2 * slot + g], send_sem=ssem.at[0], recv_sem=sem,
            device_id=(me, 1 - g), device_id_type=MESH).wait_recv()

    for d in range(1, hi):
        put(x_ref, me, (((mh + d) % hi) * lo + ml, g), ssem.at[d], rsem.at[me])
    spread(x_ref, me, 0)
    partner(x_ref, me, 0)
    local = pltpu.make_async_copy(x_ref, out_ref.at[2 * me + g], lsem)
    local.start()

    def finish():
        at = 1
        for d in range(1, hi):
            slot = ((mh + hi - d) % hi) * lo + ml
            arrived(slot, rsem.at[slot])
            spread(out_ref.at[2 * slot + g], slot, d)
            partner(out_ref.at[2 * slot + g], slot, at)
            at += 1
        for d in range(hi):
            for e in range(1, lo):
                slot = ((mh + hi - d) % hi) * lo + (ml + lo - e) % lo
                arrived(slot, rsem.at[slot])
                partner(out_ref.at[2 * slot + g], slot, at)
                at += 1
        for slot in range(blocks):
            pltpu.make_async_remote_copy(
                src_ref=x_ref, dst_ref=out_ref.at[2 * slot + 1 - g], send_sem=ssem.at[0],
                recv_sem=prsem.at[slot], device_id=(me, 1 - g), device_id_type=MESH).wait_recv()
        for copy in sends:
            copy.wait_send()
        local.wait()

    return finish


def greet(blocks):
    me = lax.axis_index("blk")
    g = lax.axis_index("grp")
    barrier = pltpu.get_barrier_semaphore()
    for o in range(1, blocks):
        pl.semaphore_signal(barrier, inc=1, device_id=((me + o) % blocks, g), device_id_type=MESH)
    pl.semaphore_signal(barrier, inc=1, device_id=(me, 1 - g), device_id_type=MESH)
    return lambda: pl.semaphore_wait(barrier, blocks)


def prepare(plan_ref, ratings_ref, bits_ref, send_ref, masked_ref, mask_ref, words_ref):
    tiles, users, width = ratings_ref.shape
    groups = WORD // 2
    span = width // groups
    own = lax.axis_index("grp")
    half_users = users // 2
    words_ref[...] = jnp.zeros_like(words_ref)
    words_ref[0:tiles, 0:users] = bits_ref[...]
    words_ref[...] = words_ref[...].T
    group_at = lax.broadcasted_iota(jnp.int32, (users, width), 1) // span + own * groups
    row_at = lax.broadcasted_iota(jnp.int32, (groups, users), 0) + own * groups
    item_at = lax.broadcasted_iota(jnp.int32, (half_users, 2 * width), 1) // span
    my_first = pl.multiple_of(own * half_users, half_users)
    mine = words_ref[pl.ds(my_first, half_users), :]
    masked_list, grouped_list = [], []
    for k in range(tiles):
        column = words_ref[0:users, k:k + 1]
        shown = (jnp.right_shift(jnp.broadcast_to(column, (users, width)), group_at) & 1).astype(F32)
        masked = ratings_ref[k].astype(F32) * shown
        masked_ref[k] = masked.astype(BF16)
        masked_list.append(masked)
        words = jnp.broadcast_to(bits_ref[k:k + 1, :], (groups, users))
        grouped_list.append((jnp.right_shift(words, row_at) & 1).astype(F32))
        seen = jnp.right_shift(jnp.broadcast_to(mine[:, k:k + 1], (half_users, 2 * width)), item_at) & 1
        mask_ref[:, k * 2 * width:(k + 1) * 2 * width] = seen.astype(F32).astype(BF16)

    def fill(o, carry):
        chosen, grouped = masked_list[0], grouped_list[0]
        for k in range(1, tiles):
            chosen = jnp.where(plan_ref[k] == o, masked_list[k], chosen)
            grouped = jnp.where(plan_ref[k] == o, grouped_list[k], grouped)
        send_ref[o, 0:users, :] = chosen.astype(BF16)
        send_ref[o, users:users + groups, 0:users] = grouped.astype(BF16)
        send_ref[o, users:users + groups, users:] = jnp.zeros((groups, width - users), BF16)
        return carry

    lax.fori_loop(1, send_ref.shape[0], fill, 0)


def user_pass(blocks, plan_ref, items_ref, mask_ref, right_ref, vt_ref, v_ref, sums_ref):
    me = lax.axis_index("blk")
    half = mask_ref.shape[0]
    width, rank = items_ref.shape[1:]
    for k in range(plan_ref.shape[0]):
        source = (me + plan_ref[k]) % blocks
        for part in range(2):
            block = items_ref[2 * source + part]
            at = (2 * k + part) * width
            v_ref[at:at + width, :] = block
            vt_ref[:, at:at + width] = block.astype(F32).T.astype(BF16)
    factors = v_ref[...]
    mask = mask_ref[...].astype(F32)
    count = jnp.sum(mask, axis=1, keepdims=True)
    ridge = ridge_scale * (count + 1.0)
    right = dot(right_ref[...], factors)
    diagonal = (lax.broadcasted_iota(jnp.int32, (rank, rank), 0)
                == lax.broadcasted_iota(jnp.int32, (rank, rank), 1)).astype(F32)
    turned = vt_ref[...]
    for u in range(half):
        weighted = turned * mask_ref[u:u + 1, :]
        gram = dot(weighted, factors) + ridge[u:u + 1, :] * diagonal
        sums_ref[u:u + 1, :] = jnp.sum(jnp.abs(gram), axis=0, keepdims=True)
    bound = jnp.max(sums_ref[0:half, :], axis=1, keepdims=True)
    return relax(factors, mask, right, count, bound)


def item_pass(blocks, plan_ref, users_ref, slots_ref, mask_ref, sums_ref):
    me = lax.axis_index("blk")
    tiles = plan_ref.shape[0]
    items, rank = sums_ref.shape
    users = 2 * users_ref.shape[1]
    groups = slots_ref.shape[1] - users
    span = items // groups
    factor_list, rating_list, mask_list = [], [], []
    for k in range(tiles):
        offset = plan_ref[k]
        source = (me + blocks - offset) % blocks
        factor_list += [users_ref[2 * source], users_ref[2 * source + 1]]
        slot = slots_ref[offset]
        rating_list.append(slot[0:users])
        mask_list.append(slot[users:users + groups, 0:users].astype(F32))
    factors = jnp.concatenate(factor_list, axis=0)
    right = dot_tn(jnp.concatenate(rating_list, axis=0), factors)
    mask_ref[...] = jnp.concatenate(mask_list, axis=1)
    turned = factors.astype(F32).T.astype(BF16)
    diagonal = (lax.broadcasted_iota(jnp.int32, (rank, rank), 0)
                == lax.broadcasted_iota(jnp.int32, (rank, rank), 1)).astype(F32)
    spread = []
    for j in range(groups):
        row = mask_ref[j:j + 1, :]
        ridge = ridge_scale * (jnp.sum(row, axis=1, keepdims=True) + 1.0)
        gram = dot(turned * row.astype(BF16), factors) + ridge * diagonal
        sums_ref[j * span:(j + 1) * span, :] = jnp.broadcast_to(
            jnp.sum(jnp.abs(gram), axis=0, keepdims=True), (span, rank))
        spread.append(jnp.broadcast_to(row, (span, row.shape[1])))
    mask = jnp.concatenate(spread, axis=0)
    count = jnp.sum(mask, axis=1, keepdims=True)
    bound = jnp.max(sums_ref[...], axis=1, keepdims=True)
    return relax(factors, mask, right, count, bound)


def whole_kernel(blocks, lo, plan_ref, start_ref, ratings_ref, bits_ref, user_ref, item_ref,
                 items_ref, users_ref, again_ref, send_ref, slots_ref, masked_ref, other_ref, mask_ref,
                 right_ref, vt_ref, v_ref, sums_ref, rows_ref, words_ref, first_ref, *sems):
    me = lax.axis_index("blk")
    g = lax.axis_index("grp")
    a_send, a_recv, m_send, m_recv = sems[15:]
    tiles, half, width = other_ref.shape
    met = greet(blocks)
    prepare(plan_ref, ratings_ref, bits_ref, send_ref, masked_ref, mask_ref, words_ref)
    met()
    finish = gather_steps(blocks, lo, start_ref, items_ref, *sems[0:5])
    swap = pltpu.make_async_remote_copy(
        src_ref=masked_ref.at[:, pl.ds(pl.multiple_of((1 - g) * half, half), half), :], dst_ref=other_ref,
        send_sem=m_send, recv_sem=m_recv, device_id=(me, 1 - g), device_id_type=MESH)
    swap.start()
    finish()
    moves = []
    for o in range(1, blocks):
        copy = pltpu.make_async_remote_copy(
            src_ref=send_ref.at[o], dst_ref=slots_ref.at[o], send_sem=a_send.at[o], recv_sem=a_recv.at[o],
            device_id=((me + o) % blocks, g), device_id_type=MESH)
        copy.start()
        moves.append(copy)
    swap.wait()
    mine = pl.multiple_of(g * half, half)
    for k in range(tiles):
        own = masked_ref[k, pl.ds(mine, half), :].astype(F32)
        far = other_ref[k].astype(F32)
        at = 2 * k * width
        right_ref[:, at:at + width] = jnp.where(g == 0, own, far).astype(BF16)
        right_ref[:, at + width:at + 2 * width] = jnp.where(g == 0, far, own).astype(BF16)
    first_ref[...] = user_pass(blocks, plan_ref, items_ref, mask_ref, right_ref, vt_ref, v_ref, sums_ref)
    gather_steps(blocks, lo, first_ref, users_ref, *sems[5:10])()
    for copy in moves:
        copy.wait()
    item_ref[...] = item_pass(blocks, plan_ref, users_ref, slots_ref, rows_ref, sums_ref)
    gather_steps(blocks, lo, item_ref, again_ref, *sems[10:15])()
    user_ref[...] = user_pass(blocks, plan_ref, again_ref, mask_ref, right_ref, vt_ref, v_ref, sums_ref)


def gather_sems(blocks, lo):
    dma = pltpu.SemaphoreType.DMA
    hi = blocks // lo
    return [dma((hi + hi * lo,)), dma((blocks,)), dma((blocks,)), dma((blocks,)), dma(())]


def body(item_start, ratings, rating_bits, plan):
    blocks = lax.axis_size("blk")
    lo = 4 if blocks % 4 == 0 else 1
    tiles, users, width = ratings.shape
    items, rank = item_start.shape
    half = users // 2
    groups = WORD // 2
    dma = pltpu.SemaphoreType.DMA
    slot = (blocks, users + groups, width)
    side = tiles * 2 * width
    return pl.pallas_call(
        functools.partial(whole_kernel, blocks, lo),
        out_shape=(jax.ShapeDtypeStruct((half, rank), BF16), jax.ShapeDtypeStruct((items, rank), BF16)),
        in_specs=[SMEM] + [VMEM] * 3, out_specs=(VMEM, VMEM),
        scratch_shapes=[
            pltpu.VMEM((2 * blocks, items, rank), BF16),
            pltpu.VMEM((2 * blocks, half, rank), BF16),
            pltpu.VMEM((2 * blocks, items, rank), BF16),
            pltpu.VMEM(slot, BF16),
            pltpu.VMEM(slot, BF16),
            pltpu.VMEM((tiles, users, width), BF16),
            pltpu.VMEM((tiles, half, width), BF16),
            pltpu.VMEM((half, side), BF16),
            pltpu.VMEM((half, side), BF16),
            pltpu.VMEM((rank, side), BF16),
            pltpu.VMEM((side, rank), BF16),
            pltpu.VMEM((items, rank), F32),
            pltpu.VMEM((groups, tiles * users), F32),
            pltpu.VMEM((128, 128), jnp.int32),
            pltpu.VMEM((half, rank), BF16),
        ] + 3 * gather_sems(blocks, lo) + [dma((blocks,)), dma((blocks,)), dma(()), dma(())],
        compiler_params=pltpu.CompilerParams(collective_id=0, has_side_effects=True),
        name="sweeps",
    )(plan, item_start, ratings, rating_bits)


def solution(mesh):
    in_specs = (P(("blk", "grp"), None), P(None, "blk", "grp"), P(None, "blk"), P())
    out_specs = (P(("blk", "grp"), None), P(("blk", "grp"), None))
    return jax.shard_map(body, mesh=mesh, in_specs=in_specs, out_specs=out_specs, check_vma=False)
```

```python
import functools
import math

import jax
import jax.numpy as jnp
from jax import lax
from jax.experimental import pallas as pl
from jax.experimental.pallas import tpu as pltpu
from jax.sharding import PartitionSpec as P

SWEEPS = 4
WORD = 32
ridge_scale = 0.005
MESH = pl.DeviceIdType.MESH
VMEM = pl.BlockSpec(memory_space=pltpu.VMEM)
SMEM = pl.BlockSpec(memory_space=pltpu.SMEM)
F32 = jnp.float32
BF16 = jnp.bfloat16


def halves(value):
    high = value.astype(BF16)
    return high, (value - high.astype(F32)).astype(BF16)


def dot(a, b):
    return jnp.dot(a, b, preferred_element_type=F32)


def dot_nt(a, b):
    return lax.dot_general(a, b, (((1,), (1,)), ((), ())), preferred_element_type=F32)


def dot_tn(a, b):
    return lax.dot_general(a, b, (((0,), (0,)), ((), ())), preferred_element_type=F32)


def product(factors, turned, mask, ridge, scale, vector):
    rows = vector.shape[0]
    seen = dot(jnp.concatenate(halves(vector), axis=0), turned)
    seen = (seen[:rows] + seen[rows:]) * mask
    applied = dot(jnp.concatenate(halves(seen), axis=0), factors)
    return (applied[:rows] + applied[rows:] + ridge * vector) * scale


def combine(powers, bound, scale):
    inverse = 1.0 / (bound * scale)
    total = None
    for j in reversed(range(SWEEPS)):
        term = powers[j] * float((-1) ** j * math.comb(SWEEPS, j + 1))
        total = (term if total is None else term + total) * inverse
    return (total * scale).astype(BF16)


def gather_steps(blocks, lo, x_ref, out_ref, ssem, rsem, psem, prsem, lsem):
    me = lax.axis_index("blk")
    g = lax.axis_index("grp")
    hi = blocks // lo
    mh, ml = me // lo, me % lo
    sends = []

    def put(src, slot, device, send_sem, recv_sem):
        copy = pltpu.make_async_remote_copy(
            src_ref=src, dst_ref=out_ref.at[2 * slot + g], send_sem=send_sem, recv_sem=recv_sem,
            device_id=device, device_id_type=MESH)
        copy.start()
        sends.append(copy)

    def spread(src, slot, d):
        for e in range(1, lo):
            put(src, slot, (mh * lo + (ml + e) % lo, g), ssem.at[hi + d * lo + e], rsem.at[slot])

    def partner(src, slot, at):
        put(src, slot, (me, 1 - g), psem.at[at], prsem.at[slot])

    def arrived(slot, sem):
        pltpu.make_async_remote_copy(
            src_ref=x_ref, dst_ref=out_ref.at[2 * slot + g], send_sem=ssem.at[0], recv_sem=sem,
            device_id=(me, 1 - g), device_id_type=MESH).wait_recv()

    for d in range(1, hi):
        put(x_ref, me, (((mh + d) % hi) * lo + ml, g), ssem.at[d], rsem.at[me])
    spread(x_ref, me, 0)
    partner(x_ref, me, 0)
    local = pltpu.make_async_copy(x_ref, out_ref.at[2 * me + g], lsem)
    local.start()

    def finish(between=None):
        at = 1
        for d in range(1, hi):
            slot = ((mh + hi - d) % hi) * lo + ml
            arrived(slot, rsem.at[slot])
            spread(out_ref.at[2 * slot + g], slot, d)
            partner(out_ref.at[2 * slot + g], slot, at)
            at += 1
        for d in range(hi):
            for e in range(1, lo):
                slot = ((mh + hi - d) % hi) * lo + (ml + lo - e) % lo
                arrived(slot, rsem.at[slot])
                partner(out_ref.at[2 * slot + g], slot, at)
                at += 1
        if between is not None:
            between()
        for slot in range(blocks):
            pltpu.make_async_remote_copy(
                src_ref=x_ref, dst_ref=out_ref.at[2 * slot + 1 - g], send_sem=ssem.at[0],
                recv_sem=prsem.at[slot], device_id=(me, 1 - g), device_id_type=MESH).wait_recv()
        local.wait()
        return sends

    return finish


def greet(blocks):
    me = lax.axis_index("blk")
    g = lax.axis_index("grp")
    barrier = pltpu.get_barrier_semaphore()
    for o in range(1, blocks):
        pl.semaphore_signal(barrier, inc=1, device_id=((me + o) % blocks, g), device_id_type=MESH)
    pl.semaphore_signal(barrier, inc=1, device_id=(me, 1 - g), device_id_type=MESH)
    return lambda: pl.semaphore_wait(barrier, blocks)


def prepare(plan_ref, ratings_ref, bits_ref, send_ref, masked_ref, mask_ref, words_ref):
    tiles, users, width = ratings_ref.shape
    groups = WORD // 2
    span = width // groups
    own = lax.axis_index("grp")
    half_users = users // 2
    words_ref[...] = jnp.zeros_like(words_ref)
    words_ref[0:tiles, 0:users] = bits_ref[...]
    words_ref[...] = words_ref[...].T
    group_at = lax.broadcasted_iota(jnp.int32, (users, width), 1) // span + own * groups
    row_at = lax.broadcasted_iota(jnp.int32, (groups, users), 0) + own * groups
    item_at = lax.broadcasted_iota(jnp.int32, (half_users, 2 * width), 1) // span
    my_first = pl.multiple_of(own * half_users, half_users)
    mine = words_ref[pl.ds(my_first, half_users), :]
    masked_list, grouped_list = [], []
    for k in range(tiles):
        column = words_ref[0:users, k:k + 1]
        shown = (jnp.right_shift(jnp.broadcast_to(column, (users, width)), group_at) & 1).astype(F32)
        masked = ratings_ref[k].astype(F32) * shown
        masked_ref[k] = masked.astype(BF16)
        masked_list.append(masked)
        words = jnp.broadcast_to(bits_ref[k:k + 1, :], (groups, users))
        grouped_list.append((jnp.right_shift(words, row_at) & 1).astype(F32))
        seen = jnp.right_shift(jnp.broadcast_to(mine[:, k:k + 1], (half_users, 2 * width)), item_at) & 1
        mask_ref[:, k * 2 * width:(k + 1) * 2 * width] = seen.astype(F32).astype(BF16)

    def fill(o, carry):
        chosen, grouped = masked_list[0], grouped_list[0]
        for k in range(1, tiles):
            chosen = jnp.where(plan_ref[k] == o, masked_list[k], chosen)
            grouped = jnp.where(plan_ref[k] == o, grouped_list[k], grouped)
        send_ref[o, 0:users, :] = chosen.astype(BF16)
        send_ref[o, users:users + groups, 0:users] = grouped.astype(BF16)
        send_ref[o, users:users + groups, users:] = jnp.zeros((groups, width - users), BF16)
        return carry

    lax.fori_loop(1, send_ref.shape[0], fill, 0)


def user_pass(blocks, plan_ref, items_ref, mask_ref, right_ref, vt_ref, v_ref, sums_ref):
    me = lax.axis_index("blk")
    half = mask_ref.shape[0]
    width, rank = items_ref.shape[1:]
    for k in range(plan_ref.shape[0]):
        source = (me + plan_ref[k]) % blocks
        for part in range(2):
            block = items_ref[2 * source + part]
            at = (2 * k + part) * width
            v_ref[at:at + width, :] = block
            vt_ref[:, at:at + width] = block.astype(F32).T.astype(BF16)
    factors = v_ref[...]
    mask = mask_ref[...].astype(F32)
    count = jnp.sum(mask, axis=1, keepdims=True)
    ridge = ridge_scale * (count + 1.0)
    right = dot(right_ref[...], factors)
    diagonal = (lax.broadcasted_iota(jnp.int32, (rank, rank), 0)
                == lax.broadcasted_iota(jnp.int32, (rank, rank), 1)).astype(F32)
    turned = vt_ref[...]
    scale = 1.0 / (count + 1.0)
    powers = [right]
    segment = max(half // SWEEPS, 1)
    for u in range(half):
        if u % segment == 0 and len(powers) < SWEEPS:
            powers.append(product(factors, turned, mask, ridge, scale, powers[-1]))
        weighted = turned * mask_ref[u:u + 1, :]
        gram = dot(weighted, factors) + ridge[u:u + 1, :] * diagonal
        sums_ref[u:u + 1, :] = jnp.sum(jnp.abs(gram), axis=0, keepdims=True)
    bound = jnp.max(sums_ref[0:half, :], axis=1, keepdims=True)
    return combine(powers, bound, scale)


def item_pass(blocks, plan_ref, users_ref, slots_ref, mask_ref, sums_ref):
    me = lax.axis_index("blk")
    tiles = plan_ref.shape[0]
    items, rank = sums_ref.shape
    users = 2 * users_ref.shape[1]
    groups = slots_ref.shape[1] - users
    span = items // groups
    factor_list, rating_list, mask_list = [], [], []
    for k in range(tiles):
        offset = plan_ref[k]
        source = (me + blocks - offset) % blocks
        factor_list += [users_ref[2 * source], users_ref[2 * source + 1]]
        slot = slots_ref[offset]
        rating_list.append(slot[0:users])
        mask_list.append(slot[users:users + groups, 0:users].astype(F32))
    factors = jnp.concatenate(factor_list, axis=0)
    right = dot_tn(jnp.concatenate(rating_list, axis=0), factors)
    mask_ref[...] = jnp.concatenate(mask_list, axis=1)
    turned = factors.astype(F32).T.astype(BF16)
    diagonal = (lax.broadcasted_iota(jnp.int32, (rank, rank), 0)
                == lax.broadcasted_iota(jnp.int32, (rank, rank), 1)).astype(F32)
    mask = jnp.concatenate([jnp.broadcast_to(mask_ref[j:j + 1, :], (span, mask_ref.shape[1])) for j in range(groups)], axis=0)
    count = jnp.sum(mask, axis=1, keepdims=True)
    scale = 1.0 / (count + 1.0)
    powers = [right]
    segment = max(groups // SWEEPS, 1)
    for j in range(groups):
        if j % segment == 0 and len(powers) < SWEEPS:
            powers.append(product(factors, turned, mask, ridge_scale * (count + 1.0), scale, powers[-1]))
        row = mask_ref[j:j + 1, :]
        ridge = ridge_scale * (jnp.sum(row, axis=1, keepdims=True) + 1.0)
        gram = dot(turned * row.astype(BF16), factors) + ridge * diagonal
        sums_ref[j * span:(j + 1) * span, :] = jnp.broadcast_to(
            jnp.sum(jnp.abs(gram), axis=0, keepdims=True), (span, rank))
    bound = jnp.max(sums_ref[...], axis=1, keepdims=True)
    return combine(powers, bound, scale)


def whole_kernel(blocks, lo, plan_ref, start_ref, ratings_hbm, bits_hbm, user_ref, item_ref,
                 ratings_ref, bits_ref,
                 items_ref, users_ref, again_ref, send_ref, slots_ref, masked_ref, other_ref, mask_ref,
                 right_ref, vt_ref, v_ref, sums_ref, rows_ref, words_ref, first_ref, *sems):
    me = lax.axis_index("blk")
    g = lax.axis_index("grp")
    a_send, a_recv, m_send, m_recv, in_sems = sems[15:]
    tiles, half, width = other_ref.shape
    met = greet(blocks)
    loads = [pltpu.make_async_copy(ratings_hbm, ratings_ref, in_sems.at[0]),
             pltpu.make_async_copy(bits_hbm, bits_ref, in_sems.at[1])]
    for load in loads:
        load.start()
    for load in loads:
        load.wait()
    prepare(plan_ref, ratings_ref, bits_ref, send_ref, masked_ref, mask_ref, words_ref)
    met()
    finish = gather_steps(blocks, lo, start_ref, items_ref, *sems[0:5])
    swap = pltpu.make_async_remote_copy(
        src_ref=masked_ref.at[:, pl.ds(pl.multiple_of((1 - g) * half, half), half), :], dst_ref=other_ref,
        send_sem=m_send, recv_sem=m_recv, device_id=(me, 1 - g), device_id_type=MESH)
    swap.start()
    moves = []

    def move():
        for o in range(1, blocks):
            copy = pltpu.make_async_remote_copy(
                src_ref=send_ref.at[o], dst_ref=slots_ref.at[o], send_sem=a_send.at[o], recv_sem=a_recv.at[o],
                device_id=((me + o) % blocks, g), device_id_type=MESH)
            copy.start()
            moves.append(copy)

    sends = finish(move)
    swap.wait()
    mine = pl.multiple_of(g * half, half)
    for k in range(tiles):
        own = masked_ref[k, pl.ds(mine, half), :].astype(F32)
        far = other_ref[k].astype(F32)
        at = 2 * k * width
        right_ref[:, at:at + width] = jnp.where(g == 0, own, far).astype(BF16)
        right_ref[:, at + width:at + 2 * width] = jnp.where(g == 0, far, own).astype(BF16)
    first_ref[...] = user_pass(blocks, plan_ref, items_ref, mask_ref, right_ref, vt_ref, v_ref, sums_ref)
    sends += gather_steps(blocks, lo, first_ref, users_ref, *sems[5:10])()
    for copy in moves:
        copy.wait_recv()
    item_ref[...] = item_pass(blocks, plan_ref, users_ref, slots_ref, rows_ref, sums_ref)
    sends += gather_steps(blocks, lo, item_ref, again_ref, *sems[10:15])()
    user_ref[...] = user_pass(blocks, plan_ref, again_ref, mask_ref, right_ref, vt_ref, v_ref, sums_ref)
    for copy in sends + moves:
        copy.wait_send()


def hand_over(user_ref, item_ref, user_out, item_out):
    user_out[...] = user_ref[...]
    item_out[...] = item_ref[...]


def gather_sems(blocks, lo):
    dma = pltpu.SemaphoreType.DMA
    hi = blocks // lo
    return [dma((hi + hi * lo,)), dma((blocks,)), dma((blocks,)), dma((blocks,)), dma(())]


def body(item_start, ratings, rating_bits, plan):
    blocks = lax.axis_size("blk")
    lo = 4 if blocks % 4 == 0 else 1
    tiles, users, width = ratings.shape
    items, rank = item_start.shape
    half = users // 2
    groups = WORD // 2
    dma = pltpu.SemaphoreType.DMA
    slot = (blocks, users + groups, width)
    side = tiles * 2 * width
    outs = (jax.ShapeDtypeStruct((half, rank), BF16), jax.ShapeDtypeStruct((items, rank), BF16))
    results = pl.pallas_call(
        functools.partial(whole_kernel, blocks, lo),
        out_shape=outs,
        in_specs=[SMEM] + [pl.BlockSpec(memory_space=pl.ANY)] * 3, out_specs=(VMEM, VMEM),
        scratch_shapes=[
            pltpu.VMEM(ratings.shape, BF16),
            pltpu.VMEM(rating_bits.shape, jnp.int32),
            pltpu.VMEM((2 * blocks, items, rank), BF16),
            pltpu.VMEM((2 * blocks, half, rank), BF16),
            pltpu.VMEM((2 * blocks, items, rank), BF16),
            pltpu.VMEM(slot, BF16),
            pltpu.VMEM(slot, BF16),
            pltpu.VMEM((tiles, users, width), BF16),
            pltpu.VMEM((tiles, half, width), BF16),
            pltpu.VMEM((half, side), BF16),
            pltpu.VMEM((half, side), BF16),
            pltpu.VMEM((rank, side), BF16),
            pltpu.VMEM((side, rank), BF16),
            pltpu.VMEM((items, rank), F32),
            pltpu.VMEM((groups, tiles * users), F32),
            pltpu.VMEM((128, 128), jnp.int32),
            pltpu.VMEM((half, rank), BF16),
        ] + 3 * gather_sems(blocks, lo) + [dma((blocks,)), dma((blocks,)), dma(()), dma(()), dma((2,))],
        compiler_params=pltpu.CompilerParams(collective_id=0, has_side_effects=True),
        name="sweeps",
    )(plan, item_start, ratings, rating_bits)
    return pl.pallas_call(
        hand_over, out_shape=outs, in_specs=[VMEM, VMEM], out_specs=(VMEM, VMEM), name="hand_over",
    )(*results)


def solution(mesh):
    in_specs = (P(("blk", "grp"), None), P(None, "blk", "grp"), P(None, "blk"), P())
    out_specs = (P(("blk", "grp"), None), P(("blk", "grp"), None))
    return jax.shard_map(body, mesh=mesh, in_specs=in_specs, out_specs=out_specs, check_vma=False)
```

```python
import functools
import math

import jax
import jax.numpy as jnp
from jax import lax
from jax.experimental import pallas as pl
from jax.experimental.pallas import tpu as pltpu
from jax.sharding import PartitionSpec as P

SWEEPS = 4
WORD = 32
ridge_scale = 0.005
MESH = pl.DeviceIdType.MESH
VMEM = pl.BlockSpec(memory_space=pltpu.VMEM)
SMEM = pl.BlockSpec(memory_space=pltpu.SMEM)
F32 = jnp.float32
BF16 = jnp.bfloat16


def halves(value):
    high = value.astype(BF16)
    return high, (value - high.astype(F32)).astype(BF16)


def dot(a, b):
    return jnp.dot(a, b, preferred_element_type=F32)


def dot_nt(a, b):
    return lax.dot_general(a, b, (((1,), (1,)), ((), ())), preferred_element_type=F32)


def dot_tn(a, b):
    return lax.dot_general(a, b, (((0,), (0,)), ((), ())), preferred_element_type=F32)


def product(factors, turned, mask, ridge, scale, vector):
    rows = vector.shape[0]
    seen = dot(jnp.concatenate(halves(vector), axis=0), turned)
    seen = (seen[:rows] + seen[rows:]) * mask
    applied = dot(jnp.concatenate(halves(seen), axis=0), factors)
    return (applied[:rows] + applied[rows:] + ridge * vector) * scale


def combine(powers, bound, scale):
    inverse = 1.0 / (bound * scale)
    total = None
    for j in reversed(range(SWEEPS)):
        term = powers[j] * float((-1) ** j * math.comb(SWEEPS, j + 1))
        total = (term if total is None else term + total) * inverse
    return (total * scale).astype(BF16)


def gather_steps(blocks, lo, x_ref, out_ref, ssem, rsem, psem, prsem, lsem):
    me = lax.axis_index("blk")
    g = lax.axis_index("grp")
    hi = blocks // lo
    mh, ml = me // lo, me % lo
    sends = []

    def put(src, slot, device, send_sem, recv_sem):
        copy = pltpu.make_async_remote_copy(
            src_ref=src, dst_ref=out_ref.at[2 * slot + g], send_sem=send_sem, recv_sem=recv_sem,
            device_id=device, device_id_type=MESH)
        copy.start()
        sends.append(copy)

    def spread(src, slot, d):
        for e in range(1, lo):
            put(src, slot, (mh * lo + (ml + e) % lo, g), ssem.at[hi + d * lo + e], rsem.at[slot])

    def partner(src, slot, at):
        put(src, slot, (me, 1 - g), psem.at[at], prsem.at[slot])

    def arrived(slot, sem):
        pltpu.make_async_remote_copy(
            src_ref=x_ref, dst_ref=out_ref.at[2 * slot + g], send_sem=ssem.at[0], recv_sem=sem,
            device_id=(me, 1 - g), device_id_type=MESH).wait_recv()

    for d in range(1, hi):
        put(x_ref, me, (((mh + d) % hi) * lo + ml, g), ssem.at[d], rsem.at[me])
    spread(x_ref, me, 0)
    partner(x_ref, me, 0)
    local = pltpu.make_async_copy(x_ref, out_ref.at[2 * me + g], lsem)
    local.start()

    def finish(between=None):
        at = 1
        for d in range(1, hi):
            slot = ((mh + hi - d) % hi) * lo + ml
            arrived(slot, rsem.at[slot])
            spread(out_ref.at[2 * slot + g], slot, d)
            partner(out_ref.at[2 * slot + g], slot, at)
            at += 1
        for d in range(hi):
            for e in range(1, lo):
                slot = ((mh + hi - d) % hi) * lo + (ml + lo - e) % lo
                arrived(slot, rsem.at[slot])
                partner(out_ref.at[2 * slot + g], slot, at)
                at += 1
        if between is not None:
            between()
        for slot in range(blocks):
            pltpu.make_async_remote_copy(
                src_ref=x_ref, dst_ref=out_ref.at[2 * slot + 1 - g], send_sem=ssem.at[0],
                recv_sem=prsem.at[slot], device_id=(me, 1 - g), device_id_type=MESH).wait_recv()
        local.wait()
        return sends

    return finish


def greet(blocks):
    me = lax.axis_index("blk")
    g = lax.axis_index("grp")
    barrier = pltpu.get_barrier_semaphore()
    for o in range(1, blocks):
        pl.semaphore_signal(barrier, inc=1, device_id=((me + o) % blocks, g), device_id_type=MESH)
    pl.semaphore_signal(barrier, inc=1, device_id=(me, 1 - g), device_id_type=MESH)
    return lambda: pl.semaphore_wait(barrier, blocks)


def prepare(plan_ref, ratings_ref, bits_ref, send_ref, masked_ref, mask_ref, words_ref):
    tiles, users, width = ratings_ref.shape
    groups = WORD // 2
    span = width // groups
    own = lax.axis_index("grp")
    half_users = users // 2
    words_ref[...] = jnp.zeros_like(words_ref)
    words_ref[0:tiles, 0:users] = bits_ref[...]
    words_ref[...] = words_ref[...].T
    group_at = lax.broadcasted_iota(jnp.int32, (users, width), 1) // span + own * groups
    row_at = lax.broadcasted_iota(jnp.int32, (groups, users), 0) + own * groups
    item_at = lax.broadcasted_iota(jnp.int32, (half_users, 2 * width), 1) // span
    my_first = pl.multiple_of(own * half_users, half_users)
    mine = words_ref[pl.ds(my_first, half_users), :]
    masked_list, grouped_list = [], []
    for k in range(tiles):
        column = words_ref[0:users, k:k + 1]
        shown = (jnp.right_shift(jnp.broadcast_to(column, (users, width)), group_at) & 1).astype(F32)
        masked = ratings_ref[k].astype(F32) * shown
        masked_ref[k] = masked.astype(BF16)
        masked_list.append(masked)
        words = jnp.broadcast_to(bits_ref[k:k + 1, :], (groups, users))
        grouped_list.append((jnp.right_shift(words, row_at) & 1).astype(F32))
        seen = jnp.right_shift(jnp.broadcast_to(mine[:, k:k + 1], (half_users, 2 * width)), item_at) & 1
        mask_ref[:, k * 2 * width:(k + 1) * 2 * width] = seen.astype(F32).astype(BF16)

    def fill(o, carry):
        chosen, grouped = masked_list[0], grouped_list[0]
        for k in range(1, tiles):
            chosen = jnp.where(plan_ref[k] == o, masked_list[k], chosen)
            grouped = jnp.where(plan_ref[k] == o, grouped_list[k], grouped)
        send_ref[o, 0:users, :] = chosen.astype(BF16)
        send_ref[o, users:users + groups, 0:users] = grouped.astype(BF16)
        send_ref[o, users:users + groups, users:] = jnp.zeros((groups, width - users), BF16)
        return carry

    lax.fori_loop(1, send_ref.shape[0], fill, 0)


def user_pass(blocks, plan_ref, items_ref, mask_ref, right_ref, vt_ref, v_ref, sums_ref):
    me = lax.axis_index("blk")
    half = mask_ref.shape[0]
    width, rank = items_ref.shape[1:]
    for k in range(plan_ref.shape[0]):
        source = (me + plan_ref[k]) % blocks
        for part in range(2):
            block = items_ref[2 * source + part]
            at = (2 * k + part) * width
            v_ref[at:at + width, :] = block
            vt_ref[:, at:at + width] = block.astype(F32).T.astype(BF16)
    factors = v_ref[...]
    mask = mask_ref[...].astype(F32)
    count = jnp.sum(mask, axis=1, keepdims=True)
    ridge = ridge_scale * (count + 1.0)
    right = dot(right_ref[...], factors)
    diagonal = (lax.broadcasted_iota(jnp.int32, (rank, rank), 0)
                == lax.broadcasted_iota(jnp.int32, (rank, rank), 1)).astype(F32)
    turned = vt_ref[...]
    scale = 1.0 / (count + 1.0)
    powers = [right]
    segment = max(half // SWEEPS, 1)
    for u in range(half):
        if u % segment == 0 and len(powers) < SWEEPS:
            powers.append(product(factors, turned, mask, ridge, scale, powers[-1]))
        weighted = turned * mask_ref[u:u + 1, :]
        gram = dot(weighted, factors) + ridge[u:u + 1, :] * diagonal
        sums_ref[u:u + 1, :] = jnp.sum(jnp.abs(gram), axis=0, keepdims=True)
    bound = jnp.max(sums_ref[0:half, :], axis=1, keepdims=True)
    return combine(powers, bound, scale)


def item_pass(blocks, plan_ref, users_ref, slots_ref, mask_ref, sums_ref):
    me = lax.axis_index("blk")
    tiles = plan_ref.shape[0]
    items, rank = sums_ref.shape
    users = 2 * users_ref.shape[1]
    groups = slots_ref.shape[1] - users
    span = items // groups
    factor_list, rating_list, mask_list = [], [], []
    for k in range(tiles):
        offset = plan_ref[k]
        source = (me + blocks - offset) % blocks
        factor_list += [users_ref[2 * source], users_ref[2 * source + 1]]
        slot = slots_ref[offset]
        rating_list.append(slot[0:users])
        mask_list.append(slot[users:users + groups, 0:users].astype(F32))
    factors = jnp.concatenate(factor_list, axis=0)
    right = dot_tn(jnp.concatenate(rating_list, axis=0), factors)
    mask_ref[...] = jnp.concatenate(mask_list, axis=1)
    turned = factors.astype(F32).T.astype(BF16)
    diagonal = (lax.broadcasted_iota(jnp.int32, (rank, rank), 0)
                == lax.broadcasted_iota(jnp.int32, (rank, rank), 1)).astype(F32)
    mask = jnp.concatenate([jnp.broadcast_to(mask_ref[j:j + 1, :], (span, mask_ref.shape[1])) for j in range(groups)], axis=0)
    count = jnp.sum(mask, axis=1, keepdims=True)
    scale = 1.0 / (count + 1.0)
    powers = [right]
    segment = max(groups // SWEEPS, 1)
    for j in range(groups):
        if j % segment == 0 and len(powers) < SWEEPS:
            powers.append(product(factors, turned, mask, ridge_scale * (count + 1.0), scale, powers[-1]))
        row = mask_ref[j:j + 1, :]
        ridge = ridge_scale * (jnp.sum(row, axis=1, keepdims=True) + 1.0)
        gram = dot(turned * row.astype(BF16), factors) + ridge * diagonal
        sums_ref[j * span:(j + 1) * span, :] = jnp.broadcast_to(
            jnp.sum(jnp.abs(gram), axis=0, keepdims=True), (span, rank))
    bound = jnp.max(sums_ref[...], axis=1, keepdims=True)
    return combine(powers, bound, scale)


def whole_kernel(blocks, lo, plan_ref, start_ref, ratings_hbm, bits_hbm, user_ref, item_ref,
                 ratings_ref, bits_ref,
                 items_ref, users_ref, again_ref, send_ref, slots_ref, masked_ref, other_ref, mask_ref,
                 right_ref, vt_ref, v_ref, sums_ref, rows_ref, words_ref, first_ref, *sems):
    me = lax.axis_index("blk")
    g = lax.axis_index("grp")
    a_send, a_recv, m_send, m_recv, in_sems = sems[15:]
    tiles, half, width = other_ref.shape
    met = greet(blocks)
    loads = [pltpu.make_async_copy(ratings_hbm, ratings_ref, in_sems.at[0]),
             pltpu.make_async_copy(bits_hbm, bits_ref, in_sems.at[1])]
    for load in loads:
        load.start()
    for load in loads:
        load.wait()
    prepare(plan_ref, ratings_ref, bits_ref, send_ref, masked_ref, mask_ref, words_ref)
    met()
    finish = gather_steps(blocks, lo, start_ref, items_ref, *sems[0:5])
    swap = pltpu.make_async_remote_copy(
        src_ref=masked_ref.at[:, pl.ds(pl.multiple_of((1 - g) * half, half), half), :], dst_ref=other_ref,
        send_sem=m_send, recv_sem=m_recv, device_id=(me, 1 - g), device_id_type=MESH)
    swap.start()
    moves = []

    def move():
        for o in range(1, blocks):
            copy = pltpu.make_async_remote_copy(
                src_ref=send_ref.at[o], dst_ref=slots_ref.at[o], send_sem=a_send.at[o], recv_sem=a_recv.at[o],
                device_id=((me + o) % blocks, g), device_id_type=MESH)
            copy.start()
            moves.append(copy)

    sends = finish(move)
    swap.wait()
    mine = pl.multiple_of(g * half, half)
    for k in range(tiles):
        own = masked_ref[k, pl.ds(mine, half), :].astype(F32)
        far = other_ref[k].astype(F32)
        at = 2 * k * width
        right_ref[:, at:at + width] = jnp.where(g == 0, own, far).astype(BF16)
        right_ref[:, at + width:at + 2 * width] = jnp.where(g == 0, far, own).astype(BF16)
    first_ref[...] = user_pass(blocks, plan_ref, items_ref, mask_ref, right_ref, vt_ref, v_ref, sums_ref)
    sends += gather_steps(blocks, blocks, first_ref, users_ref, *sems[5:10])()
    for copy in moves:
        copy.wait_recv()
    item_ref[...] = item_pass(blocks, plan_ref, users_ref, slots_ref, rows_ref, sums_ref)
    sends += gather_steps(blocks, lo, item_ref, again_ref, *sems[10:15])()
    user_ref[...] = user_pass(blocks, plan_ref, again_ref, mask_ref, right_ref, vt_ref, v_ref, sums_ref)
    for copy in sends + moves:
        copy.wait_send()


def hand_over(user_ref, item_ref, user_out, item_out):
    user_out[...] = user_ref[...]
    item_out[...] = item_ref[...]


def gather_sems(blocks, lo):
    dma = pltpu.SemaphoreType.DMA
    hi = blocks // lo
    return [dma((hi + hi * lo,)), dma((blocks,)), dma((blocks,)), dma((blocks,)), dma(())]


def body(item_start, ratings, rating_bits, plan):
    blocks = lax.axis_size("blk")
    lo = 4 if blocks % 4 == 0 else 1
    tiles, users, width = ratings.shape
    items, rank = item_start.shape
    half = users // 2
    groups = WORD // 2
    dma = pltpu.SemaphoreType.DMA
    slot = (blocks, users + groups, width)
    side = tiles * 2 * width
    outs = (jax.ShapeDtypeStruct((half, rank), BF16), jax.ShapeDtypeStruct((items, rank), BF16))
    results = pl.pallas_call(
        functools.partial(whole_kernel, blocks, lo),
        out_shape=outs,
        in_specs=[SMEM] + [pl.BlockSpec(memory_space=pl.ANY)] * 3, out_specs=(VMEM, VMEM),
        scratch_shapes=[
            pltpu.VMEM(ratings.shape, BF16),
            pltpu.VMEM(rating_bits.shape, jnp.int32),
            pltpu.VMEM((2 * blocks, items, rank), BF16),
            pltpu.VMEM((2 * blocks, half, rank), BF16),
            pltpu.VMEM((2 * blocks, items, rank), BF16),
            pltpu.VMEM(slot, BF16),
            pltpu.VMEM(slot, BF16),
            pltpu.VMEM((tiles, users, width), BF16),
            pltpu.VMEM((tiles, half, width), BF16),
            pltpu.VMEM((half, side), BF16),
            pltpu.VMEM((half, side), BF16),
            pltpu.VMEM((rank, side), BF16),
            pltpu.VMEM((side, rank), BF16),
            pltpu.VMEM((items, rank), F32),
            pltpu.VMEM((groups, tiles * users), F32),
            pltpu.VMEM((128, 128), jnp.int32),
            pltpu.VMEM((half, rank), BF16),
        ] + gather_sems(blocks, lo) + gather_sems(blocks, blocks) + gather_sems(blocks, lo) + [dma((blocks,)), dma((blocks,)), dma(()), dma(()), dma((2,))],
        compiler_params=pltpu.CompilerParams(collective_id=0, has_side_effects=True),
        name="sweeps",
    )(plan, item_start, ratings, rating_bits)
    return pl.pallas_call(
        hand_over, out_shape=outs, in_specs=[VMEM, VMEM], out_specs=(VMEM, VMEM), name="hand_over",
    )(*results)


def solution(mesh):
    in_specs = (P(("blk", "grp"), None), P(None, "blk", "grp"), P(None, "blk"), P())
    out_specs = (P(("blk", "grp"), None), P(("blk", "grp"), None))
    return jax.shard_map(body, mesh=mesh, in_specs=in_specs, out_specs=out_specs, check_vma=False)
```
